128 devices in a mesh: field: 2 (over x_lo), row: 8 (over z, core), col: 8 (over x_hi, y).
Axes of the slice: x: 4 (x_hi: 2, x_lo: 2; x = x_hi * 2 + x_lo), y: 4, z: 4, core: 2. Of those that a mesh axis runs over, the one named last changes fastest.
Arguments:
- init_state: float32 [2, 4, 2048, 4096], P('field', None, 'row', 'col'), may hold values from 0 to 2
- cond_x: float32 [2, 4, 2048, 4096], P('field', None, 'row', 'col'), may hold values from 0.2 to 2
- cond_y: float32 [2, 4, 2048, 4096], P('field', None, 'row', 'col'), may hold values from 0.2 to 2
- activity: float32 [2, 2048, 4096], P('field', 'row', 'col'), may hold values from 0.5 to 1.5
- power_class: int32 [2, 2048, 4096], P('field', 'row', 'col'), may hold values from 0 to 7
- class_table: float32 [2, 8], P('field'), may hold values from 0.25 to 2
- via_mask: int32 [2, 3, 2048, 4096], P('field', None, 'row', 'col'), may hold values 0 or 1
Outputs:
- final_state: float32 [2, 4, 2048, 4096], P('field', None, 'row', 'col')
The draws below stay inside these ranges and needn't reach their ends.
All inputs are finite; a program needn't handle non-finite values. No bound on the sum of `via_mask` on one device may be relied on, other than what follows from the above.
Results may differ from the reference program's by a relative error of at most 0.00002.
Values sent between devices are 32-bit elements; how exact they have to be, the bound alone decides.
A program may use at most 128 MiB of HBM per device.

```python
import math
import jax
import jax.numpy as jnp

PLANES = 4
CLASSES = 8
SWEEPS = 4
STEPS = 2
HALVES = 2
NROWS = 2048
NCOLS = 4096


def place_ends(drawn, key, least, high):
    index_at = [jax.random.randint(jax.random.fold_in(key, axis), (), 0, length) for axis, length in enumerate(drawn.shape)]
    main_axis = drawn.shape.index(max(drawn.shape))
    next_to = index_at[:main_axis] + [(index_at[main_axis] + 1) % drawn.shape[main_axis]] + index_at[main_axis + 1:]
    return drawn.at[tuple(index_at)].set(least).at[tuple(next_to)].set(high)


def level_of(stream_key, dims, shards, least, top_value):
    def one(axis_at, parts):
        heights = jax.random.uniform(jax.random.fold_in(jax.random.fold_in(stream_key, 6), axis_at), (parts,), jnp.float32, least / len(shards), top_value / len(shards))
        return jnp.repeat(jnp.exp(heights), dims[axis_at] // parts).reshape((-1,) + (1,) * (len(dims) - axis_at - 1))

    gain = one(*shards[0])
    for cut in shards[1:]:
        gain = gain * one(*cut)
    return gain


def setup_inputs(seed: int = 0) -> dict:
    streams_of = jax.random.split(jax.random.key(seed), 8)
    return {
        "init_state": jnp.clip(2.0 * jax.random.uniform(streams_of[0], (HALVES, PLANES, NROWS, NCOLS), jnp.float32) ** level_of(streams_of[0], (HALVES, PLANES, NROWS, NCOLS), ((0, 2), (2, 8), (3, 8)), -0.2, 0.2), 0.0, 2.0),
        "cond_x": jnp.clip(jnp.exp(math.log(2.0) - 2.3025851 * jax.random.uniform(streams_of[1], (HALVES, PLANES, NROWS, NCOLS), jnp.float32) ** level_of(streams_of[1], (HALVES, PLANES, NROWS, NCOLS), ((0, 2), (2, 8), (3, 8)), -0.2, 0.2)), 0.2, 2.0),
        "cond_y": jnp.clip(jnp.exp(math.log(2.0) - 2.3025851 * jax.random.uniform(streams_of[2], (HALVES, PLANES, NROWS, NCOLS), jnp.float32) ** level_of(streams_of[2], (HALVES, PLANES, NROWS, NCOLS), ((0, 2), (2, 8), (3, 8)), -0.2, 0.2)), 0.2, 2.0),
        "activity": jnp.clip(0.5 + 1.0 * jax.random.uniform(streams_of[3], (HALVES, NROWS, NCOLS), jnp.float32) ** level_of(streams_of[3], (HALVES, NROWS, NCOLS), ((0, 2), (1, 8), (2, 8)), -0.2, 0.2), 0.5, 1.5),
        "power_class": place_ends(jax.random.randint(streams_of[4], (HALVES, NROWS, NCOLS), 0, CLASSES), jax.random.fold_in(streams_of[4], 1), 0, CLASSES - 1).astype(jnp.int32),
        "class_table": jnp.clip(jnp.exp(math.log(2.0) - 2.0794415 * jax.random.uniform(streams_of[5], (HALVES, CLASSES), jnp.float32) ** level_of(streams_of[5], (HALVES, CLASSES), ((0, 2),), -0.2, 0.2)), 0.25, 2.0),
        "via_mask": place_ends((jax.random.randint(streams_of[6], (HALVES, 3, NROWS, NCOLS), 0, 2) < 1).astype(jnp.int32), jax.random.fold_in(streams_of[6], 1), 0, 1),
    }


LEAK = 0.05
VIA_G = 1.0
TEMP_COEF = 0.5
HEAT_SCALE = 1.0


def from_east(field_in):
    return jnp.pad(field_in, ((0, 0), (0, 0), (0, 1)))[:, :, 1:]


def from_west(field_in):
    return jnp.pad(field_in, ((0, 0), (0, 0), (1, 0)))[:, :, :-1]


def from_south(field_in):
    return jnp.pad(field_in, ((0, 0), (0, 1), (0, 0)))[:, 1:, :]


def from_north(field_in):
    return jnp.pad(field_in, ((0, 0), (1, 0), (0, 0)))[:, :-1, :]


def face_east(kappa):
    keep = (jnp.arange(kappa.shape[2]) < kappa.shape[2] - 1).astype(jnp.float32)
    return 0.5 * (kappa + from_east(kappa)) * keep[None, None, :]


def face_south(kappa):
    keep = (jnp.arange(kappa.shape[1]) < kappa.shape[1] - 1).astype(jnp.float32)
    return 0.5 * (kappa + from_south(kappa)) * keep[None, :, None]


def joule_map(state, cond_east, cond_south):
    heat = cond_east * (state - from_east(state)) ** 2 + cond_south * (state - from_south(state)) ** 2
    return jnp.stack([heat[0] + heat[3], heat[1] + heat[2]])


def sweep_once(state, cond_east, cond_south, source, vertical):
    cond_west = from_west(cond_east)
    cond_north = from_north(cond_south)
    zero_plane = jnp.zeros_like(state[:1])
    link_up = jnp.concatenate([zero_plane, vertical], 0)
    link_down = jnp.concatenate([vertical, zero_plane], 0)
    above = jnp.concatenate([zero_plane, state[:-1]], 0)
    below = jnp.concatenate([state[1:], zero_plane], 0)
    total = (source + cond_east * from_east(state) + cond_west * from_west(state)
             + cond_south * from_south(state) + cond_north * from_north(state)
             + link_up * above + link_down * below)
    weight = cond_east + cond_west + cond_south + cond_north + link_up + link_down + LEAK
    return total / weight


def reference(init_state, cond_x, cond_y, activity, power_class, class_table, via_mask):
    plane_map = jnp.array([0, 1, 1, 0], jnp.int32)
    selects = [jnp.array([0.0, 1.0, 1.0, 0.0], jnp.float32), jnp.array([0.0, 1.0, 0.0, 0.0], jnp.float32)]
    faces = [jnp.array([1.0, 0.0, 1.0], jnp.float32), jnp.array([1.0, 1.0, 1.0], jnp.float32)]
    bases = []
    verticals = []
    for half in range(2):
        load = jnp.take(class_table[half], power_class[half], axis=0) * activity[half]
        bases.append(selects[half][:, None, None] * load[None])
        verticals.append(via_mask[half].astype(jnp.float32) * VIA_G * faces[half][:, None, None])
    states = [init_state[0], init_state[1]]
    for step_index in range(STEPS):
        joule = joule_map(states[0], cond_x[0], cond_y[0])
        temps = states[1][0:2]
        factor = 1.0 / (1.0 + TEMP_COEF * temps[plane_map])
        coupled = [
            (face_east(cond_x[0] * factor), face_south(cond_y[0] * factor), bases[0]),
            (face_east(cond_x[1]), face_south(cond_y[1]),
             bases[1] + HEAT_SCALE * jnp.concatenate([joule, jnp.zeros_like(joule)], 0)),
        ]
        new_states = []
        for half in range(2):
            current = states[half]
            for sweep_index in range(SWEEPS):
                current = sweep_once(current, coupled[half][0], coupled[half][1], coupled[half][2], verticals[half])
            new_states.append(current)
        states = new_states
    return jnp.stack(states)
```

```python
import functools

import jax
import jax.numpy as jnp
from jax import lax
from jax.experimental import pallas as pl
from jax.experimental.pallas import tpu as pltpu
from jax.sharding import PartitionSpec as P

MESH = pl.DeviceIdType.MESH
F32 = jnp.float32
SWEEPS = 4
STEPS = 2
LEAK = 0.05
TEMP_COEF = 0.5

LANES = 128
HALO = 8
GUARD = 8
R = 16
STRIP = 8
PACKED = 16


def kernel(
    grid_rows, grid_cols,
    state_in, cx_in, cy_in, act_in, class_in, table, via_in, out,
    x, y, z, cx, cy, ce, cs, rw, ky, vert, load, src, act, cls, via,
    send_map, recv_map, pack_send, pack_recv,
    load_sem, row_send_sem, row_recv_sem, col_send_sem, col_recv_sem,
    map_send_sem, map_recv_sem, out_sem,
):
    rows, cols = state_in.shape[2], state_in.shape[3]
    tiles = cols // LANES
    wide = rows + 2 * HALO
    chunks = wide // R
    field = lax.axis_index("field")
    row = lax.axis_index("row")
    col = lax.axis_index("col")
    is_elec = field == 0
    has_n, has_s = row > 0, row < grid_rows - 1
    has_w, has_e = col > 0, col < grid_cols - 1
    lane = lax.broadcasted_iota(jnp.int32, (1, LANES), 1)
    lane3 = lax.broadcasted_iota(jnp.int32, (1, 1, LANES), 2)
    arrays = (
        (state_in, x, GUARD), (cx_in, cx, GUARD), (cy_in, cy, GUARD),
        (via_in, via, 0), (act_in, act, 0), (class_in, cls, 0),
    )

    def lanes_of(t):
        return pl.ds(pl.multiple_of(t * LANES, LANES), LANES)

    def pick(item, first, dest, count, t):
        source, target, base = item
        spot = pl.ds(base + dest, count)
        if len(source.shape) == 4:
            return source.at[0, :, pl.ds(first, count), lanes_of(t)], target.at[:, t, spot, :]
        return source.at[0, pl.ds(first, count), lanes_of(t)], target.at[t, spot, :]

    def local_copy(k, t):
        a, b = pick(arrays[k], 0, HALO, rows, t)
        return pltpu.make_async_copy(a, b, load_sem.at[k, t])

    def row_copy(k, t, down):
        first, dest = (rows - HALO, 0) if down else (0, rows + HALO)
        a, b = pick(arrays[k], first, dest, HALO, t)
        return pltpu.make_async_remote_copy(
            src_ref=a, dst_ref=b,
            send_sem=row_send_sem.at[int(down), k, t], recv_sem=row_recv_sem.at[int(down), k, t],
            device_id={"row": row + 1 if down else row - 1}, device_id_type=MESH,
        )

    def each_tile(action):
        def body(t, carry):
            for k in range(len(arrays)):
                action(k, t)
            return carry
        lax.fori_loop(0, tiles, body, 0)

    each_tile(lambda k, t: local_copy(k, t).start())

    barrier = pltpu.get_barrier_semaphore()
    pl.semaphore_signal(barrier, inc=1, device_id={"field": 1 - field}, device_id_type=MESH)
    for dr, has_r in ((-1, has_n), (0, None), (1, has_s)):
        for dc, has_c in ((-1, has_w), (0, None), (1, has_e)):
            if dr == 0 and dc == 0:
                continue
            there = has_c if has_r is None else has_r if has_c is None else has_r & has_c

            @pl.when(there)
            def _(dr=dr, dc=dc):
                pl.semaphore_signal(
                    barrier, inc=1, device_id={"row": row + dr, "col": col + dc}, device_id_type=MESH
                )
    near_r = 1 + has_n.astype(jnp.int32) + has_s.astype(jnp.int32)
    near_c = 1 + has_w.astype(jnp.int32) + has_e.astype(jnp.int32)
    pl.semaphore_wait(barrier, near_r * near_c)

    @pl.when(has_n)
    def _():
        each_tile(lambda k, t: row_copy(k, t, False).start())

    @pl.when(has_s)
    def _():
        each_tile(lambda k, t: row_copy(k, t, True).start())

    def clear_rows(dest):
        for source, target, base in arrays:
            spot = pl.ds(base + dest, HALO)
            if len(source.shape) == 4:
                target[:, 0:tiles, spot, :] = jnp.zeros(
                    (target.shape[0], tiles, HALO, LANES), target.dtype)
            else:
                target[:, spot, :] = jnp.zeros((tiles, HALO, LANES), target.dtype)

    @pl.when(jnp.logical_not(has_n))
    def _():
        clear_rows(0)

    @pl.when(jnp.logical_not(has_s))
    def _():
        clear_rows(rows + HALO)

    def prepare(first, count, t):
        spot = pl.ds(first, count)
        spot_g = pl.ds(first + GUARD, count)
        ids = cls[t, spot, :]
        density = jnp.where(ids == 1, table[0, 1], table[0, 0])
        for k in range(2, table.shape[1]):
            density = jnp.where(ids == k, table[0, k], density)
        load[t, spot_g, :] = density * act[t, spot, :]
        for q in range(3):
            vert[q, t, spot_g, :] = via[q, t, spot, :].astype(F32)

    each_tile(lambda k, t: local_copy(k, t).wait())

    def prepare_tile(t, carry):
        def body(i, carry):
            prepare(pl.multiple_of(HALO + i * 32, 8), 32, t)
            return carry
        return lax.fori_loop(0, rows // 32, body, carry)
    lax.fori_loop(0, tiles, prepare_tile, 0)

    def plane_at(q, t, spot):
        if q < 4:
            return x, (q, t, spot, slice(None))
        if q < 8:
            return cx, (q - 4, t, spot, slice(None))
        if q < 12:
            return cy, (q - 8, t, spot, slice(None))
        if q == 12:
            return load, (t, spot, slice(None))
        return vert, (q - 13, t, spot, slice(None))

    group = lane // 8

    def pack(i, carry):
        first = pl.multiple_of(i * 32, 32)
        spot = pl.ds(first + GUARD + HALO, 32)
        west = jnp.zeros((32, LANES), F32)
        east = jnp.zeros((32, LANES), F32)
        for q in range(PACKED):
            ref, index = plane_at(q, 0, spot)
            west = jnp.where(group == q, pltpu.roll(ref[index], 8 * q, 1) if q else ref[index], west)
            ref, index = plane_at(q, tiles - 1, spot)
            shift = (8 * q + 8) % LANES
            east = jnp.where(group == q, pltpu.roll(ref[index], shift, 1) if shift else ref[index], east)
        pack_send[0, pl.ds(first, 32), :] = west
        pack_send[1, pl.ds(first, 32), :] = east
        return carry
    lax.fori_loop(0, rows // 32, pack, 0)

    def col_copy(side, dr):
        first, dest, count = ((0, rows + HALO, HALO), (0, HALO, rows), (rows - HALO, 0, HALO))[dr + 1]
        return pltpu.make_async_remote_copy(
            src_ref=pack_send.at[side, pl.ds(first, count), :],
            dst_ref=pack_recv.at[side, pl.ds(dest, count), :],
            send_sem=col_send_sem.at[side, dr + 1], recv_sem=col_recv_sem.at[side, dr + 1],
            device_id={"row": row + dr, "col": col + (1 if side else -1)}, device_id_type=MESH,
        )

    def each_side(action, incoming):
        for side in range(2):
            for dr in (0, -1, 1):
                has_c = (has_w, has_e)[1 - side if incoming else side]
                step = -dr if incoming else dr
                there = has_c if step == 0 else has_c & (has_n if step < 0 else has_s)
                action(side, dr, there)

    def send_side(side, dr, there):
        @pl.when(there)
        def _():
            col_copy(side, dr).start()

    each_side(send_side, False)

    @pl.when(has_s)
    def _():
        each_tile(lambda k, t: row_copy(k, t, False).wait_recv())

    @pl.when(has_n)
    def _():
        each_tile(lambda k, t: row_copy(k, t, True).wait_recv())

    def prepare_edge(t, carry):
        prepare(0, HALO, t)
        prepare(rows + HALO, HALO, t)
        return carry
    lax.fori_loop(0, tiles, prepare_edge, 0)

    def recv_side(side, dr, there):
        _, dest, count = ((0, rows + HALO, HALO), (0, HALO, rows), (0, 0, HALO))[dr + 1]

        @pl.when(there)
        def _():
            col_copy(side, dr).wait_recv()

        @pl.when(jnp.logical_not(there))
        def _():
            pack_recv[side, pl.ds(dest, count), :] = jnp.zeros((count, LANES), F32)

    each_side(recv_side, True)

    def unpack(c, carry):
        first = pl.multiple_of(c * R, R)
        spot = pl.ds(first + GUARD, R)
        east = pack_recv[0, pl.ds(first, R), :]
        west = pack_recv[1, pl.ds(first, R), :]
        for q in range(PACKED):
            e = pltpu.roll(east, LANES - 8 * q, 1) if q else east
            shift = (120 - 8 * q) % LANES
            w = pltpu.roll(west, shift, 1) if shift else west
            ref, index = plane_at(q, tiles, spot)
            ref[index] = jnp.where(lane < 64, e, w)
        return carry
    lax.fori_loop(0, chunks, unpack, 0)

    def from_east(v):
        r = pltpu.roll(v, LANES - 1, 2)
        return jnp.where(lane3 == LANES - 1, jnp.concatenate([r[1:], r[:1]], 0), r)

    def from_west(v):
        r = pltpu.roll(v, 1, 2)
        return jnp.where(lane3 == 0, jnp.concatenate([r[-1:], r[:-1]], 0), r)

    def at(first):
        return pl.ds(first + GUARD, R)

    def half_east():
        tile = lax.broadcasted_iota(jnp.int32, (tiles + 1, 1, LANES), 0)
        closed = (lane3 == LANES - 1) & (
            ((tile == tiles - 1) & jnp.logical_not(has_e)) | ((tile == tiles) & jnp.logical_not(has_w)))
        return jnp.where(closed, 0.0, 0.5).astype(F32)

    def half_south(first):
        at_row = first + lax.broadcasted_iota(jnp.int32, (1, R, LANES), 1)
        closed = ((at_row == HALO - 1) & jnp.logical_not(has_n)) | (
            (at_row == HALO + rows - 1) & jnp.logical_not(has_s))
        return jnp.where(closed, 0.0, 0.5).astype(F32)

    def links_of(p, elec, first):
        if elec:
            return vert[0 if p < 2 else 2, :, at(first), :]
        if p == 0:
            return vert[0, :, at(first), :]
        if p == 3:
            return vert[2, :, at(first), :]
        return vert[p - 1, :, at(first), :] + vert[p, :, at(first), :]

    def face_rows(first, elec):
        kappa = ky if elec else cy
        here, above = half_south(first), half_south(first - 1)
        for p in range(4):
            k = kappa[p, :, at(first), :]
            south = here * (k + kappa[p, :, at(first + 1), :])
            north = above * (k + kappa[p, :, at(first - 1), :])
            east = ce[p, :, at(first), :]
            cs[p, :, at(first), :] = south
            weight = east + from_west(east) + south + north + links_of(p, elec, first) + LEAK
            rw[p, :, at(first), :] = 1.0 / weight

    def sweep(old, new, first, elec):
        for p in range(4):
            v = old[p, :, at(first), :]
            east = ce[p, :, at(first), :]
            total = east * from_east(v) + from_west(east * v)
            total = total + cs[p, :, at(first), :] * old[p, :, at(first + 1), :]
            total = total + cs[p, :, at(first - 1), :] * old[p, :, at(first - 1), :]
            if elec:
                total = total + vert[0 if p < 2 else 2, :, at(first), :] * old[p ^ 1, :, at(first), :]
                if p in (1, 2):
                    total = total + load[:, at(first), :]
            else:
                if p > 0:
                    total = total + vert[p - 1, :, at(first), :] * old[p - 1, :, at(first), :]
                if p < 3:
                    total = total + vert[p, :, at(first), :] * old[p + 1, :, at(first), :]
                if p < 2:
                    total = total + src[p, :, at(first), :]
            new[p, :, at(first), :] = total * rw[p, :, at(first), :]

    strip_group = lane // 16

    def write_map(step, c, planes):
        strip = jnp.zeros((STRIP, LANES), F32)
        for q in range(2):
            send_map[step, c, pl.ds(q * tiles * R, tiles * R), :] = planes[q][:tiles].reshape(tiles * R, LANES)
            for b in range(R // 8):
                k = 2 * b + q
                strip = jnp.where(
                    strip_group == k, pltpu.roll(planes[q][tiles, 8 * b : 8 * b + 8], 8 + 16 * k, 1), strip)
        send_map[step, c, pl.ds(2 * tiles * R, STRIP), :] = strip

    def read_map(step, c):
        strip = recv_map[step, c, pl.ds(2 * tiles * R, STRIP), :]
        planes = []
        for q in range(2):
            main = recv_map[step, c, pl.ds(q * tiles * R, tiles * R), :].reshape(tiles, R, LANES)
            parts = [pltpu.roll(strip, LANES - (8 + 16 * (2 * b + q)), 1) for b in range(R // 8)]
            planes.append(jnp.concatenate([main, jnp.concatenate(parts, 0)[None]], 0))
        return planes

    def map_copy(step, c):
        return pltpu.make_async_remote_copy(
            src_ref=send_map.at[step, c], dst_ref=recv_map.at[step, c],
            send_sem=map_send_sem.at[step, c], recv_sem=map_recv_sem.at[step, c],
            device_id={"field": 1 - field}, device_id_type=MESH,
        )

    def send_chunk(step, c, state):
        first = pl.multiple_of(c * R, R)

        @pl.when(is_elec)
        def _():
            heats = []
            for p in range(4):
                v = state[p, :, at(first), :]
                de = v - from_east(v)
                ds = v - state[p, :, at(first + 1), :]
                heats.append(cx[p, :, at(first), :] * (de * de) + cy[p, :, at(first), :] * (ds * ds))
            write_map(step, c, (heats[0] + heats[3], heats[1] + heats[2]))

        @pl.when(jnp.logical_not(is_elec))
        def _():
            write_map(step, c, (state[0, :, at(first), :], state[1, :, at(first), :]))

        map_copy(step, c).start()

    def first_maps(c, carry):
        send_chunk(0, c, x)
        return carry
    lax.fori_loop(0, chunks, first_maps, 0)

    @pl.when(jnp.logical_not(is_elec))
    def _():
        def body(c, carry):
            first = pl.multiple_of(c * R, R)
            he = half_east()
            for p in range(4):
                k = cx[p, :, at(first), :]
                ce[p, :, at(first), :] = he * (k + from_east(k))
            face_rows(first - 1, False)
            return carry
        lax.fori_loop(0, chunks, body, 0)

    def advance(step, c, buffers):
        first = pl.multiple_of(c * R, R)
        map_copy(step, c).wait_recv()

        @pl.when(is_elec)
        def _():
            temps = read_map(step, c)
            factor = [1.0 / (1.0 + TEMP_COEF * t) for t in temps]
            he = half_east()
            for p in range(4):
                f = factor[(0, 1, 1, 0)[p]]
                k = cx[p, :, at(first), :] * f
                ce[p, :, at(first), :] = he * (k + from_east(k))
                ky[p, :, at(first), :] = cy[p, :, at(first), :] * f
            face_rows(first - 1, True)
            for s in range(SWEEPS):
                sweep(buffers[s], buffers[s + 1], first - 1 - s, True)

        @pl.when(jnp.logical_not(is_elec))
        def _():
            joule = read_map(step, c)
            src[0, :, at(first), :] = joule[0]
            src[1, :, at(first), :] = joule[1] + load[:, at(first), :]
            for s in range(SWEEPS):
                sweep(buffers[s], buffers[s + 1], first - 1 - s, False)

    def step_one(c, carry):
        @pl.when(c < chunks)
        def _():
            advance(0, c, (x, y, z, y, z))

        @pl.when(c > 0)
        def _():
            send_chunk(1, c - 1, z)
        return carry
    lax.fori_loop(0, chunks + 1, step_one, 0)

    def out_copy(c, t):
        return pltpu.make_async_copy(
            x.at[:, t, pl.ds(pl.multiple_of(c * R + GUARD + HALO, 8), R), :],
            out.at[0, :, pl.ds(pl.multiple_of(c * R, R), R), lanes_of(t)],
            out_sem.at[c, t],
        )

    def step_two(c, carry):
        advance(1, c, (z, y, x, y, x))

        @pl.when(c > 0)
        def _():
            for t in range(tiles):
                out_copy(c - 1, t).start()
        return carry
    lax.fori_loop(0, chunks, step_two, 0)

    def finish(c, carry):
        for step in range(STEPS):
            map_copy(step, c).wait_send()

        @pl.when(c > 0)
        def _():
            for t in range(tiles):
                out_copy(c - 1, t).wait()
        return carry
    lax.fori_loop(0, chunks, finish, 0)

    @pl.when(has_n)
    def _():
        each_tile(lambda k, t: row_copy(k, t, False).wait_send())

    @pl.when(has_s)
    def _():
        each_tile(lambda k, t: row_copy(k, t, True).wait_send())

    def sent_side(side, dr, there):
        @pl.when(there)
        def _():
            col_copy(side, dr).wait_send()

    each_side(sent_side, False)


def shards(grid_rows, grid_cols, *args):
    rows, cols = args[0].shape[2], args[0].shape[3]
    tiles = cols // LANES
    wide = rows + 2 * HALO
    chunks = wide // R
    tall = wide + 2 * GUARD
    field = pltpu.VMEM((4, tiles + 1, tall, LANES), F32)
    message = 2 * tiles * R + STRIP
    dma = pltpu.SemaphoreType.DMA
    hbm = pl.BlockSpec(memory_space=pl.ANY)
    return pl.pallas_call(
        functools.partial(kernel, grid_rows, grid_cols),
        name="coupled_sweeps",
        out_shape=jax.ShapeDtypeStruct(args[0].shape, F32),
        in_specs=[hbm] * 5 + [pl.BlockSpec(memory_space=pltpu.SMEM), hbm],
        out_specs=hbm,
        scratch_shapes=[
            *[field] * 9,
            pltpu.VMEM((3, tiles + 1, tall, LANES), F32),
            pltpu.VMEM((tiles + 1, tall, LANES), F32),
            pltpu.VMEM((2, tiles + 1, tall, LANES), F32),
            pltpu.VMEM((tiles, wide, LANES), F32),
            pltpu.VMEM((tiles, wide, LANES), jnp.int32),
            pltpu.VMEM((3, tiles, wide, LANES), jnp.int32),
            pltpu.VMEM((STEPS, chunks, message, LANES), F32),
            pltpu.VMEM((STEPS, chunks, message, LANES), F32),
            pltpu.VMEM((2, rows, LANES), F32),
            pltpu.VMEM((2, wide, LANES), F32),
            dma((6, tiles)), dma((2, 6, tiles)), dma((2, 6, tiles)), dma((2, 3)), dma((2, 3)),
            dma((STEPS, chunks)), dma((STEPS, chunks)), dma((chunks, tiles)),
        ],
        compiler_params=pltpu.CompilerParams(
            collective_id=0, has_side_effects=True, vmem_limit_bytes=60 * 1024 * 1024
        ),
    )(*args)


def solution(mesh):
    return jax.shard_map(
        functools.partial(shards, mesh.shape["row"], mesh.shape["col"]),
        mesh=mesh,
        in_specs=(
            P("field", None, "row", "col"),
            P("field", None, "row", "col"),
            P("field", None, "row", "col"),
            P("field", "row", "col"),
            P("field", "row", "col"),
            P("field", None),
            P("field", None, "row", "col"),
        ),
        out_specs=P("field", None, "row", "col"),
        check_vma=False,
    )
```

```python
import functools

import jax
import jax.numpy as jnp
from jax import lax
from jax.experimental import pallas as pl
from jax.experimental.pallas import tpu as pltpu
from jax.sharding import PartitionSpec as P

MESH = pl.DeviceIdType.MESH
F32 = jnp.float32
SWEEPS = 4
LEAK = 0.05
TEMP_COEF = 0.5

LANES = 128
HALO = 8
GUARD = 8
R = 16
STRIP = 4
EARLY = 6
PACKED = 16


def kernel(
    grid_rows, grid_cols,
    state_in, cx_in, cy_in, act_in, class_in, table, via_in, out,
    x, y, z, cx, cy, ce, cs, rw, ky, vert, load, src, act, cls, via,
    send_main, recv_main, send_strip, recv_strip, send_map, recv_map, pack_send, pack_recv,
    load_sem, row_send_sem, row_recv_sem, col_send_sem, col_recv_sem,
    main_send_sem, main_recv_sem, strip_sem, map_send_sem, map_recv_sem, out_sem,
):
    rows, cols = state_in.shape[2], state_in.shape[3]
    tiles = cols // LANES
    wide = rows + 2 * HALO
    chunks = wide // R
    field = lax.axis_index("field")
    row = lax.axis_index("row")
    col = lax.axis_index("col")
    is_elec = field == 0
    has_n, has_s = row > 0, row < grid_rows - 1
    has_w, has_e = col > 0, col < grid_cols - 1
    lane = lax.broadcasted_iota(jnp.int32, (1, LANES), 1)
    lane3 = lax.broadcasted_iota(jnp.int32, (1, 1, LANES), 2)
    arrays = (
        (state_in, x, GUARD), (cx_in, cx, GUARD), (cy_in, cy, GUARD),
        (via_in, via, 0), (act_in, act, 0), (class_in, cls, 0),
    )

    def lanes_of(t):
        return pl.ds(pl.multiple_of(t * LANES, LANES), LANES)

    def pick(item, first, dest, count, t):
        source, target, base = item
        spot = pl.ds(base + dest, count)
        if len(source.shape) == 4:
            return source.at[0, :, pl.ds(first, count), lanes_of(t)], target.at[:, t, spot, :]
        return source.at[0, pl.ds(first, count), lanes_of(t)], target.at[t, spot, :]

    def local_copy(k, t):
        a, b = pick(arrays[k], 0, HALO, rows, t)
        return pltpu.make_async_copy(a, b, load_sem.at[k])

    def whole(k, dest, count):
        source, target, base = arrays[k]
        spot = pl.ds(base + dest, count)
        if len(source.shape) == 4:
            return target.at[:, pl.ds(0, tiles), spot, :]
        return target.at[:, spot, :]

    def wait_for(ref, sem):
        pltpu.make_async_copy(ref, ref, sem).wait()

    def loaded(*ks):
        for k in ks:
            wait_for(whole(k, HALO, rows), load_sem.at[k])

    def rows_done(sem, down):
        for k in range(len(arrays)):
            wait_for(whole(k, 0 if down else rows + HALO, HALO), sem.at[int(down), k])

    def row_copy(k, t, down):
        first, dest = (rows - HALO, 0) if down else (0, rows + HALO)
        a, b = pick(arrays[k], first, dest, HALO, t)
        return pltpu.make_async_remote_copy(
            src_ref=a, dst_ref=b,
            send_sem=row_send_sem.at[int(down), k], recv_sem=row_recv_sem.at[int(down), k],
            device_id={"row": row + 1 if down else row - 1}, device_id_type=MESH,
        )

    def each_tile(action):
        def body(t, carry):
            for k in range(len(arrays)):
                action(k, t)
            return carry
        lax.fori_loop(0, tiles, body, 0)

    def load_tiles(t, carry, ks):
        for k in ks:
            local_copy(k, t).start()
        return carry
    for ks in ((0, 1, 2), (3, 4, 5)):
        lax.fori_loop(0, tiles, functools.partial(load_tiles, ks=ks), 0)

    barrier = pltpu.get_barrier_semaphore()
    pl.semaphore_signal(barrier, inc=1, device_id={"field": 1 - field}, device_id_type=MESH)
    for dr, has_r in ((-1, has_n), (0, None), (1, has_s)):
        for dc, has_c in ((-1, has_w), (0, None), (1, has_e)):
            if dr == 0 and dc == 0:
                continue
            there = has_c if has_r is None else has_r if has_c is None else has_r & has_c

            @pl.when(there)
            def _(dr=dr, dc=dc):
                pl.semaphore_signal(
                    barrier, inc=1, device_id={"row": row + dr, "col": col + dc}, device_id_type=MESH
                )
    def clear_rows(dest):
        for source, target, base in arrays:
            spot = pl.ds(base + dest, HALO)
            if len(source.shape) == 4:
                target[:, 0:tiles, spot, :] = jnp.zeros(
                    (target.shape[0], tiles, HALO, LANES), target.dtype)
            else:
                target[:, spot, :] = jnp.zeros((tiles, HALO, LANES), target.dtype)

    @pl.when(jnp.logical_not(has_n))
    def _():
        clear_rows(0)

    @pl.when(jnp.logical_not(has_s))
    def _():
        clear_rows(rows + HALO)

    def prepare(first, count, t):
        spot = pl.ds(first, count)
        spot_g = pl.ds(first + GUARD, count)
        ids = cls[t, spot, :]
        density = jnp.where(ids == 1, table[0, 1], table[0, 0])
        for k in range(2, table.shape[1]):
            density = jnp.where(ids == k, table[0, k], density)
        load[t, spot_g, :] = density * act[t, spot, :]
        for q in range(3):
            vert[q, t, spot_g, :] = via[q, t, spot, :].astype(F32)

    loaded(0, 1, 2)

    def from_east(v):
        r = pltpu.roll(v, LANES - 1, 2)
        return jnp.where(lane3 == LANES - 1, jnp.concatenate([r[1:], r[:1]], 0), r)

    def from_west(v):
        r = pltpu.roll(v, 1, 2)
        return jnp.where(lane3 == 0, jnp.concatenate([r[-1:], r[:-1]], 0), r)

    def at(first):
        return pl.ds(first + GUARD, R)

    strip_group = lane // 16

    def heat_of(state, first, low, count):
        heats = []
        for p in range(4):
            v = state[p, low : low + count, at(first), :]
            follow = state[p, (low + count) % (tiles + 1), at(first), :][None]
            r = pltpu.roll(jnp.concatenate([v, follow], 0), LANES - 1, 2)
            de = v - jnp.where(lane3 == LANES - 1, r[1:], r[:-1])
            ds = v - state[p, low : low + count, at(first + 1), :]
            heats.append(cx[p, low : low + count, at(first), :] * (de * de)
                         + cy[p, low : low + count, at(first), :] * (ds * ds))
        return heats[0] + heats[3], heats[1] + heats[2]

    def strip_of(planes):
        full = jnp.zeros((8, LANES), F32)
        for q in range(2):
            for b in range(R // 8):
                k = 2 * b + q
                full = jnp.where(
                    lane // 32 == k, pltpu.roll(planes[q][8 * b : 8 * b + 8], (8 + 32 * k) % LANES, 1), full)
        return jnp.where(strip_group % 2 == 1, pltpu.roll(full[4:8], 16, 1), full[0:4])

    def planes_of(strip):
        full = jnp.concatenate([strip, pltpu.roll(strip, LANES - 16, 1)], 0)
        return [
            jnp.concatenate(
                [pltpu.roll(full, (LANES - 8 - 32 * (2 * b + q)) % LANES, 1) for b in range(R // 8)], 0)
            for q in range(2)
        ]

    half = tiles * R

    def first_main(c):
        first = pl.multiple_of(c * R, R)

        @pl.when(is_elec)
        def _():
            heat = heat_of(x, first, 0, tiles)
            for q in range(2):
                send_main[c, q * half : (q + 1) * half, :] = heat[q].reshape(half, LANES)

        @pl.when(jnp.logical_not(is_elec))
        def _():
            for q in range(2):
                send_main[c, q * half : (q + 1) * half, :] = x[q, 0:tiles, at(first), :].reshape(half, LANES)

    def first_strip(c):
        first = pl.multiple_of(c * R, R)

        @pl.when(is_elec)
        def _():
            heat = heat_of(x, first, tiles - 1, 2)
            send_strip[c] = strip_of([jnp.where(lane == 120, pltpu.roll(h[0], LANES - 7, 1), h[1]) for h in heat])

        @pl.when(jnp.logical_not(is_elec))
        def _():
            send_strip[c] = strip_of([x[q, tiles, at(first), :] for q in range(2)])

    def main_copy(c):
        return pltpu.make_async_remote_copy(
            src_ref=send_main.at[c], dst_ref=recv_main.at[c],
            send_sem=main_send_sem.at[0], recv_sem=main_recv_sem.at[c],
            device_id={"field": 1 - field}, device_id_type=MESH,
        )

    strip_copy = pltpu.make_async_remote_copy(
        src_ref=send_strip, dst_ref=recv_strip, send_sem=strip_sem.at[0], recv_sem=strip_sem.at[1],
        device_id={"field": 1 - field}, device_id_type=MESH,
    )

    def loop(low, high, action):
        def body(c, carry):
            action(c)
            return carry
        lax.fori_loop(low, high, body, 0)

    early = min(EARLY, chunks - 2)
    loop(1, chunks - 1, first_main)

    loaded(3, 4, 5)

    def prepare_tile(t, carry):
        def body(i, carry):
            prepare(pl.multiple_of(HALO + i * 32, 8), 32, t)
            return carry
        return lax.fori_loop(0, rows // 32, body, carry)
    lax.fori_loop(0, tiles, prepare_tile, 0)

    def plane_at(q, t, spot):
        if q < 4:
            return x, (q, t, spot, slice(None))
        if q < 8:
            return cx, (q - 4, t, spot, slice(None))
        if q < 12:
            return cy, (q - 8, t, spot, slice(None))
        if q == 12:
            return load, (t, spot, slice(None))
        return vert, (q - 13, t, spot, slice(None))

    group = lane // 8

    def pack(i, carry):
        first = pl.multiple_of(i * 32, 32)
        spot = pl.ds(first + GUARD + HALO, 32)
        west = jnp.zeros((32, LANES), F32)
        east = jnp.zeros((32, LANES), F32)
        for q in range(PACKED):
            ref, index = plane_at(q, 0, spot)
            west = jnp.where(group == q, pltpu.roll(ref[index], 8 * q, 1) if q else ref[index], west)
            ref, index = plane_at(q, tiles - 1, spot)
            shift = (8 * q + 8) % LANES
            east = jnp.where(group == q, pltpu.roll(ref[index], shift, 1) if shift else ref[index], east)
        pack_send[0, pl.ds(first, 32), :] = west
        pack_send[1, pl.ds(first, 32), :] = east
        return carry
    lax.fori_loop(0, rows // 32, pack, 0)

    def col_copy(side, dr):
        first, dest, count = ((0, rows + HALO, HALO), (0, HALO, rows), (rows - HALO, 0, HALO))[dr + 1]
        return pltpu.make_async_remote_copy(
            src_ref=pack_send.at[side, pl.ds(first, count), :],
            dst_ref=pack_recv.at[side, pl.ds(dest, count), :],
            send_sem=col_send_sem.at[side, dr + 1], recv_sem=col_recv_sem.at[side, dr + 1],
            device_id={"row": row + dr, "col": col + (1 if side else -1)}, device_id_type=MESH,
        )

    def each_side(action, incoming):
        for side in range(2):
            for dr in (0, -1, 1):
                has_c = (has_w, has_e)[1 - side if incoming else side]
                step = -dr if incoming else dr
                there = has_c if step == 0 else has_c & (has_n if step < 0 else has_s)
                action(side, dr, there)

    def send_side(side, dr, there):
        @pl.when(there)
        def _():
            col_copy(side, dr).start()

    near_r = 1 + has_n.astype(jnp.int32) + has_s.astype(jnp.int32)
    near_c = 1 + has_w.astype(jnp.int32) + has_e.astype(jnp.int32)
    pl.semaphore_wait(barrier, near_r * near_c)
    each_side(send_side, False)

    @pl.when(has_n)
    def _():
        each_tile(lambda k, t: row_copy(k, t, False).start())

    @pl.when(has_s)
    def _():
        each_tile(lambda k, t: row_copy(k, t, True).start())

    loop(1, 1 + early, lambda c: main_copy(c).start())

    @pl.when(has_s)
    def _():
        rows_done(row_recv_sem, False)

    @pl.when(has_n)
    def _():
        rows_done(row_recv_sem, True)

    def prepare_edge(t, carry):
        prepare(0, HALO, t)
        prepare(rows + HALO, HALO, t)
        return carry
    lax.fori_loop(0, tiles, prepare_edge, 0)

    def recv_side(side, dr, there):
        _, dest, count = ((0, rows + HALO, HALO), (0, HALO, rows), (0, 0, HALO))[dr + 1]

        @pl.when(there)
        def _():
            col_copy(side, dr).wait_recv()

        @pl.when(jnp.logical_not(there))
        def _():
            pack_recv[side, pl.ds(dest, count), :] = jnp.zeros((count, LANES), F32)

    each_side(recv_side, True)

    def unpack(c, carry):
        first = pl.multiple_of(c * R, R)
        spot = pl.ds(first + GUARD, R)
        east = pack_recv[0, pl.ds(first, R), :]
        west = pack_recv[1, pl.ds(first, R), :]
        for q in range(PACKED):
            e = pltpu.roll(east, LANES - 8 * q, 1) if q else east
            shift = (120 - 8 * q) % LANES
            w = pltpu.roll(west, shift, 1) if shift else west
            ref, index = plane_at(q, tiles, spot)
            ref[index] = jnp.where(lane < 64, e, w)
        return carry
    lax.fori_loop(0, chunks, unpack, 0)

    def half_east():
        tile = lax.broadcasted_iota(jnp.int32, (tiles + 1, 1, LANES), 0)
        closed = (lane3 == LANES - 1) & (
            ((tile == tiles - 1) & jnp.logical_not(has_e)) | ((tile == tiles) & jnp.logical_not(has_w)))
        return jnp.where(closed, 0.0, 0.5).astype(F32)

    def half_south(first):
        at_row = first + lax.broadcasted_iota(jnp.int32, (1, R, LANES), 1)
        closed = ((at_row == HALO - 1) & jnp.logical_not(has_n)) | (
            (at_row == HALO + rows - 1) & jnp.logical_not(has_s))
        return jnp.where(closed, 0.0, 0.5).astype(F32)

    def links_of(p, elec, first):
        if elec:
            return vert[0 if p < 2 else 2, :, at(first), :]
        if p == 0:
            return vert[0, :, at(first), :]
        if p == 3:
            return vert[2, :, at(first), :]
        return vert[p - 1, :, at(first), :] + vert[p, :, at(first), :]

    def face_rows(first, elec):
        kappa = ky if elec else cy
        here, above = half_south(first), half_south(first - 1)
        for p in range(4):
            k = kappa[p, :, at(first), :]
            south = here * (k + kappa[p, :, at(first + 1), :])
            north = above * (k + kappa[p, :, at(first - 1), :])
            east = ce[p, :, at(first), :]
            cs[p, :, at(first), :] = south
            weight = east + from_west(east) + south + north + links_of(p, elec, first) + LEAK
            rw[p, :, at(first), :] = 1.0 / weight

    def sweep(old, new, first, elec):
        for p in range(4):
            v = old[p, :, at(first), :]
            east = ce[p, :, at(first), :]
            total = east * from_east(v) + from_west(east * v)
            total = total + cs[p, :, at(first), :] * old[p, :, at(first + 1), :]
            total = total + cs[p, :, at(first - 1), :] * old[p, :, at(first - 1), :]
            if elec:
                total = total + vert[0 if p < 2 else 2, :, at(first), :] * old[p ^ 1, :, at(first), :]
                if p in (1, 2):
                    total = total + load[:, at(first), :]
            else:
                if p > 0:
                    total = total + vert[p - 1, :, at(first), :] * old[p - 1, :, at(first), :]
                if p < 3:
                    total = total + vert[p, :, at(first), :] * old[p + 1, :, at(first), :]
                if p < 2:
                    total = total + src[p, :, at(first), :]
            new[p, :, at(first), :] = total * rw[p, :, at(first), :]

    def send_chunk(c, state):
        first = pl.multiple_of(c * R, R)

        def write(planes):
            for q in range(2):
                send_map[c, q * half : (q + 1) * half, :] = planes[q][:tiles].reshape(half, LANES)
            send_map[c, 2 * half : 2 * half + STRIP, :] = strip_of([planes[q][tiles] for q in range(2)])

        @pl.when(is_elec)
        def _():
            write(heat_of(state, first, 0, tiles + 1))

        @pl.when(jnp.logical_not(is_elec))
        def _():
            write((state[0, :, at(first), :], state[1, :, at(first), :]))

        map_copy(c).start()

    def map_copy(c):
        return pltpu.make_async_remote_copy(
            src_ref=send_map.at[c], dst_ref=recv_map.at[c],
            send_sem=map_send_sem.at[c], recv_sem=map_recv_sem.at[c],
            device_id={"field": 1 - field}, device_id_type=MESH,
        )

    def read_map(step, c):
        source = recv_map if step else recv_main
        strip = recv_map[c, 2 * half : 2 * half + STRIP, :] if step else recv_strip[c]
        return [
            jnp.concatenate([source[c, q * half : (q + 1) * half, :].reshape(tiles, R, LANES), edge[None]], 0)
            for q, edge in enumerate(planes_of(strip))
        ]

    first_main(0)
    loop(0, chunks, first_strip)
    main_copy(0).start()
    strip_copy.start()
    first_main(chunks - 1)
    loop(1 + early, chunks, lambda c: main_copy(c).start())

    @pl.when(jnp.logical_not(is_elec))
    def _():
        def body(c, carry):
            first = pl.multiple_of(c * R, R)
            he = half_east()
            for p in range(4):
                k = cx[p, :, at(first), :]
                ce[p, :, at(first), :] = he * (k + from_east(k))
            face_rows(first - 1, False)
            return carry
        lax.fori_loop(0, chunks, body, 0)

    def advance(step, c, buffers):
        first = pl.multiple_of(c * R, R)
        (map_copy if step else main_copy)(c).wait_recv()

        @pl.when(is_elec)
        def _():
            temps = read_map(step, c)
            factor = [1.0 / (1.0 + TEMP_COEF * t) for t in temps]
            he = half_east()
            for p in range(4):
                f = factor[(0, 1, 1, 0)[p]]
                k = cx[p, :, at(first), :] * f
                ce[p, :, at(first), :] = he * (k + from_east(k))
                ky[p, :, at(first), :] = cy[p, :, at(first), :] * f
            face_rows(first - 1, True)
            for s in range(SWEEPS):
                sweep(buffers[s], buffers[s + 1], first - 1 - s, True)

        @pl.when(jnp.logical_not(is_elec))
        def _():
            joule = read_map(step, c)
            if step == 0:
                tile = lax.broadcasted_iota(jnp.int32, (tiles + 1, 1, LANES), 0)
                last = (tile == tiles - 1) & (lane3 == LANES - 1)
                joule = [jnp.where(last, pltpu.roll(j[tiles:], 7, 2), j) for j in joule]
            src[0, :, at(first), :] = joule[0]
            src[1, :, at(first), :] = joule[1] + load[:, at(first), :]
            for s in range(SWEEPS):
                sweep(buffers[s], buffers[s + 1], first - 1 - s, False)

    strip_copy.wait_recv()

    def step_one(c, carry):
        @pl.when(c < chunks)
        def _():
            advance(0, c, (x, y, z, y, z))

        @pl.when(c > 0)
        def _():
            send_chunk(c - 1, z)
        return carry
    lax.fori_loop(0, chunks + 1, step_one, 0)

    def out_copy(c, t):
        return pltpu.make_async_copy(
            x.at[:, t, pl.ds(pl.multiple_of(c * R + GUARD + HALO, 8), R), :],
            out.at[0, :, pl.ds(pl.multiple_of(c * R, R), R), lanes_of(t)],
            out_sem.at[0],
        )

    def step_two(c, carry):
        advance(1, c, (z, y, x, y, x))

        @pl.when(c > 0)
        def _():
            for t in range(tiles):
                out_copy(c - 1, t).start()
        return carry
    lax.fori_loop(0, chunks, step_two, 0)

    wait_for(out, out_sem.at[0])
    wait_for(send_main, main_send_sem.at[0])
    strip_copy.wait_send()
    loop(0, chunks, lambda c: map_copy(c).wait_send())

    @pl.when(has_n)
    def _():
        rows_done(row_send_sem, False)

    @pl.when(has_s)
    def _():
        rows_done(row_send_sem, True)

    def sent_side(side, dr, there):
        @pl.when(there)
        def _():
            col_copy(side, dr).wait_send()

    each_side(sent_side, False)


def shards(grid_rows, grid_cols, *args):
    rows, cols = args[0].shape[2], args[0].shape[3]
    tiles = cols // LANES
    wide = rows + 2 * HALO
    chunks = wide // R
    tall = wide + 2 * GUARD
    field = pltpu.VMEM((4, tiles + 1, tall, LANES), F32)
    dma = pltpu.SemaphoreType.DMA
    hbm = pl.BlockSpec(memory_space=pl.ANY)
    return pl.pallas_call(
        functools.partial(kernel, grid_rows, grid_cols),
        name="coupled_sweeps",
        out_shape=jax.ShapeDtypeStruct(args[0].shape, F32),
        in_specs=[hbm] * 5 + [pl.BlockSpec(memory_space=pltpu.SMEM), hbm],
        out_specs=hbm,
        scratch_shapes=[
            *[field] * 9,
            pltpu.VMEM((3, tiles + 1, tall, LANES), F32),
            pltpu.VMEM((tiles + 1, tall, LANES), F32),
            pltpu.VMEM((2, tiles + 1, tall, LANES), F32),
            pltpu.VMEM((tiles, wide, LANES), F32),
            pltpu.VMEM((tiles, wide, LANES), jnp.int32),
            pltpu.VMEM((3, tiles, wide, LANES), jnp.int32),
            *[pltpu.VMEM((chunks, 2 * tiles * R, LANES), F32)] * 2,
            *[pltpu.VMEM((chunks, STRIP, LANES), F32)] * 2,
            *[pltpu.VMEM((chunks, 2 * tiles * R + STRIP, LANES), F32)] * 2,
            pltpu.VMEM((2, rows, LANES), F32),
            pltpu.VMEM((2, wide, LANES), F32),
            dma((6,)), dma((2, 6)), dma((2, 6)), dma((2, 3)), dma((2, 3)),
            dma((1,)), dma((chunks,)), dma((2,)), dma((chunks,)), dma((chunks,)), dma((1,)),
        ],
        compiler_params=pltpu.CompilerParams(
            collective_id=0, has_side_effects=True, vmem_limit_bytes=60 * 1024 * 1024
        ),
    )(*args)


def solution(mesh):
    return jax.shard_map(
        functools.partial(shards, mesh.shape["row"], mesh.shape["col"]),
        mesh=mesh,
        in_specs=(
            P("field", None, "row", "col"),
            P("field", None, "row", "col"),
            P("field", None, "row", "col"),
            P("field", "row", "col"),
            P("field", "row", "col"),
            P("field", None),
            P("field", None, "row", "col"),
        ),
        out_specs=P("field", None, "row", "col"),
        check_vma=False,
    )
```

```python
import functools
import math

import jax
import jax.numpy as jnp
from jax import lax
from jax.experimental import pallas as pl
from jax.experimental.pallas import tpu as pltpu
from jax.sharding import PartitionSpec as P

MESH = pl.DeviceIdType.MESH
F32 = jnp.float32
SWEEPS = 4
LEAK = 0.05
TEMP_COEF = 0.5

LANES = 128
HALO = 8
GUARD = 8
R = 16
STRIP = 4
EARLY = 6
FIRST = 4
GROUP = 6
PACKED = 16


def kernel(
    grid_rows, grid_cols,
    state_in, cx_in, cy_in, act_in, class_in, table, via_in, out,
    x, y, z, cx, cy, ce, cs, rw, ky, vert, load, src, act, cls, via,
    send_main, recv_main, send_strip, recv_strip, send_map, recv_map, pack_send, pack_recv,
    load_sem, row_send_sem, row_recv_sem, col_send_sem, col_recv_sem,
    main_send_sem, main_recv_sem, strip_sem, map_send_sem, map_recv_sem, out_sem,
):
    rows, cols = state_in.shape[2], state_in.shape[3]
    tiles = cols // LANES
    wide = rows + 2 * HALO
    chunks = wide // R
    field = lax.axis_index("field")
    row = lax.axis_index("row")
    col = lax.axis_index("col")
    is_elec = field == 0
    has_n, has_s = row > 0, row < grid_rows - 1
    has_w, has_e = col > 0, col < grid_cols - 1
    lane = lax.broadcasted_iota(jnp.int32, (1, LANES), 1)
    lane3 = lax.broadcasted_iota(jnp.int32, (1, 1, LANES), 2)
    arrays = (
        (state_in, x, GUARD), (cx_in, cx, GUARD), (cy_in, cy, GUARD),
        (via_in, via, 0), (act_in, act, 0), (class_in, cls, 0),
    )

    def lanes_of(t):
        return pl.ds(pl.multiple_of(t * LANES, LANES), LANES)

    def pick(item, first, dest, count, t):
        source, target, base = item
        spot = pl.ds(base + dest, count)
        if len(source.shape) == 4:
            return source.at[0, :, pl.ds(first, count), lanes_of(t)], target.at[:, t, spot, :]
        return source.at[0, pl.ds(first, count), lanes_of(t)], target.at[t, spot, :]

    def local_copy(k, t):
        a, b = pick(arrays[k], 0, HALO, rows, t)
        return pltpu.make_async_copy(a, b, load_sem.at[k])

    def whole(k, dest, count):
        source, target, base = arrays[k]
        spot = pl.ds(base + dest, count)
        if len(source.shape) == 4:
            return target.at[:, pl.ds(0, tiles), spot, :]
        return target.at[:, spot, :]

    def wait_for(ref, sem):
        pltpu.make_async_copy(ref, ref, sem).wait()

    def loaded(*ks):
        for k in ks:
            wait_for(whole(k, HALO, rows), load_sem.at[k])

    def rows_done(sem, down):
        for k in range(len(arrays)):
            wait_for(whole(k, 0 if down else rows + HALO, HALO), sem.at[int(down), k])

    def row_copy(k, t, down):
        first, dest = (rows - HALO, 0) if down else (0, rows + HALO)
        a, b = pick(arrays[k], first, dest, HALO, t)
        return pltpu.make_async_remote_copy(
            src_ref=a, dst_ref=b,
            send_sem=row_send_sem.at[int(down), k], recv_sem=row_recv_sem.at[int(down), k],
            device_id={"row": row + 1 if down else row - 1}, device_id_type=MESH,
        )

    def each_tile(action):
        def body(t, carry):
            for k in range(len(arrays)):
                action(k, t)
            return carry
        lax.fori_loop(0, tiles, body, 0)

    def load_tiles(t, carry, ks):
        for k in ks:
            local_copy(k, t).start()
        return carry
    for ks in ((0, 1, 2), (3, 4, 5)):
        lax.fori_loop(0, tiles, functools.partial(load_tiles, ks=ks), 0)

    barrier = pltpu.get_barrier_semaphore()
    pl.semaphore_signal(barrier, inc=1, device_id={"field": 1 - field}, device_id_type=MESH)
    for dr, has_r in ((-1, has_n), (0, None), (1, has_s)):
        for dc, has_c in ((-1, has_w), (0, None), (1, has_e)):
            if dr == 0 and dc == 0:
                continue
            there = has_c if has_r is None else has_r if has_c is None else has_r & has_c

            @pl.when(there)
            def _(dr=dr, dc=dc):
                pl.semaphore_signal(
                    barrier, inc=1, device_id={"row": row + dr, "col": col + dc}, device_id_type=MESH
                )
    def clear_rows(dest):
        for source, target, base in arrays:
            spot = pl.ds(base + dest, HALO)
            if len(source.shape) == 4:
                target[:, 0:tiles, spot, :] = jnp.zeros(
                    (target.shape[0], tiles, HALO, LANES), target.dtype)
            else:
                target[:, spot, :] = jnp.zeros((tiles, HALO, LANES), target.dtype)

    @pl.when(jnp.logical_not(has_n))
    def _():
        clear_rows(0)

    @pl.when(jnp.logical_not(has_s))
    def _():
        clear_rows(rows + HALO)

    def prepare(first, count, t):
        spot = pl.ds(first, count)
        spot_g = pl.ds(first + GUARD, count)
        ids = cls[t, spot, :]
        density = jnp.where(ids == 1, table[0, 1], table[0, 0])
        for k in range(2, table.shape[1]):
            density = jnp.where(ids == k, table[0, k], density)
        load[t, spot_g, :] = density * act[t, spot, :]
        for q in range(3):
            vert[q, t, spot_g, :] = via[q, t, spot, :].astype(F32)

    loaded(0, 1, 2)

    def from_east(v):
        r = pltpu.roll(v, LANES - 1, 2)
        return jnp.where(lane3 == LANES - 1, jnp.concatenate([r[1:], r[:1]], 0), r)

    def from_west(v):
        r = pltpu.roll(v, 1, 2)
        return jnp.where(lane3 == 0, jnp.concatenate([r[-1:], r[:-1]], 0), r)

    def at(first, count=R):
        return pl.ds(first + GUARD, count)

    strip_group = lane // 16

    def heat_of(state, first, low, count, n=R):
        heats = []
        for p in range(4):
            v = state[p, low : low + count, at(first, n), :]
            follow = state[p, (low + count) % (tiles + 1), at(first, n), :][None]
            r = pltpu.roll(jnp.concatenate([v, follow], 0), LANES - 1, 2)
            de = v - jnp.where(lane3 == LANES - 1, r[1:], r[:-1])
            ds = v - state[p, low : low + count, at(first + 1, n), :]
            heats.append(cx[p, low : low + count, at(first, n), :] * (de * de)
                         + cy[p, low : low + count, at(first, n), :] * (ds * ds))
        return heats[0] + heats[3], heats[1] + heats[2]

    def strip_of(planes):
        full = jnp.zeros((8, LANES), F32)
        for q in range(2):
            for b in range(R // 8):
                k = 2 * b + q
                full = jnp.where(
                    lane // 32 == k, pltpu.roll(planes[q][8 * b : 8 * b + 8], (8 + 32 * k) % LANES, 1), full)
        return jnp.where(strip_group % 2 == 1, pltpu.roll(full[4:8], 16, 1), full[0:4])

    def planes_of(strip):
        full = jnp.concatenate([strip, pltpu.roll(strip, LANES - 16, 1)], 0)
        return [
            jnp.concatenate(
                [pltpu.roll(full, (LANES - 8 - 32 * (2 * b + q)) % LANES, 1) for b in range(R // 8)], 0)
            for q in range(2)
        ]

    half = tiles * R

    def first_main(c):
        first = pl.multiple_of(c * R, R)

        @pl.when(is_elec)
        def _():
            heat = heat_of(x, first, 0, tiles)
            for q in range(2):
                send_main[c, q * half : (q + 1) * half, :] = heat[q].reshape(half, LANES)

        @pl.when(jnp.logical_not(is_elec))
        def _():
            for q in range(2):
                send_main[c, q * half : (q + 1) * half, :] = x[q, 0:tiles, at(first), :].reshape(half, LANES)

    def first_strips():
        group = min(GROUP, chunks)
        starts = [min(c, chunks - group) for c in range(0, chunks, group)]

        def make(planes_at):
            for start in starts:
                planes = planes_at(start * R, group * R)
                for c in range(group):
                    send_strip[start + c] = strip_of([plane[c * R : (c + 1) * R] for plane in planes])

        @pl.when(is_elec)
        def _():
            def edges(first, n):
                heat = heat_of(x, first, tiles - 1, 2, n)
                return [jnp.where(lane == 120, pltpu.roll(h[0], LANES - 7, 1), h[1]) for h in heat]
            make(edges)

        @pl.when(jnp.logical_not(is_elec))
        def _():
            make(lambda first, n: [x[q, tiles, at(first, n), :] for q in range(2)])

    def main_copy(c):
        return pltpu.make_async_remote_copy(
            src_ref=send_main.at[c], dst_ref=recv_main.at[c],
            send_sem=main_send_sem.at[0], recv_sem=main_recv_sem.at[c],
            device_id={"field": 1 - field}, device_id_type=MESH,
        )

    strip_copy = pltpu.make_async_remote_copy(
        src_ref=send_strip, dst_ref=recv_strip, send_sem=strip_sem.at[0], recv_sem=strip_sem.at[1],
        device_id={"field": 1 - field}, device_id_type=MESH,
    )

    def loop(low, high, action):
        def body(c, carry):
            action(c)
            return carry
        lax.fori_loop(low, high, body, 0)

    early = min(EARLY, chunks - 2)
    ready = min(FIRST, early)
    loop(1, 1 + ready, first_main)

    loaded(3, 4, 5)

    def prepare_tile(t, carry):
        def body(i, carry):
            prepare(pl.multiple_of(HALO + i * 32, 8), 32, t)
            return carry
        return lax.fori_loop(0, rows // 32, body, carry)
    lax.fori_loop(0, tiles, prepare_tile, 0)

    def plane_at(q, t, spot):
        if q < 4:
            return x, (q, t, spot, slice(None))
        if q < 8:
            return cx, (q - 4, t, spot, slice(None))
        if q < 12:
            return cy, (q - 8, t, spot, slice(None))
        if q == 12:
            return load, (t, spot, slice(None))
        return vert, (q - 13, t, spot, slice(None))

    group = lane // 8

    deep = math.gcd(rows, 64)

    def pack(i, carry):
        first = pl.multiple_of(i * deep, deep)
        spot = pl.ds(first + GUARD + HALO, deep)
        west = jnp.zeros((deep, LANES), F32)
        east = jnp.zeros((deep, LANES), F32)
        for q in range(PACKED):
            ref, index = plane_at(q, 0, spot)
            west = jnp.where(group == q, pltpu.roll(ref[index], 8 * q, 1) if q else ref[index], west)
            ref, index = plane_at(q, tiles - 1, spot)
            shift = (8 * q + 8) % LANES
            east = jnp.where(group == q, pltpu.roll(ref[index], shift, 1) if shift else ref[index], east)
        pack_send[0, pl.ds(first, deep), :] = west
        pack_send[1, pl.ds(first, deep), :] = east
        return carry
    lax.fori_loop(0, rows // deep, pack, 0)

    def col_copy(side, dr):
        first, dest, count = ((0, rows + HALO, HALO), (0, HALO, rows), (rows - HALO, 0, HALO))[dr + 1]
        return pltpu.make_async_remote_copy(
            src_ref=pack_send.at[side, pl.ds(first, count), :],
            dst_ref=pack_recv.at[side, pl.ds(dest, count), :],
            send_sem=col_send_sem.at[side, dr + 1], recv_sem=col_recv_sem.at[side, dr + 1],
            device_id={"row": row + dr, "col": col + (1 if side else -1)}, device_id_type=MESH,
        )

    def each_side(action, incoming):
        for side in range(2):
            for dr in (0, -1, 1):
                has_c = (has_w, has_e)[1 - side if incoming else side]
                step = -dr if incoming else dr
                there = has_c if step == 0 else has_c & (has_n if step < 0 else has_s)
                action(side, dr, there)

    def send_side(side, dr, there):
        @pl.when(there)
        def _():
            col_copy(side, dr).start()

    near_r = 1 + has_n.astype(jnp.int32) + has_s.astype(jnp.int32)
    near_c = 1 + has_w.astype(jnp.int32) + has_e.astype(jnp.int32)
    pl.semaphore_wait(barrier, near_r * near_c)
    each_side(send_side, False)
    loop(1, 1 + ready, lambda c: main_copy(c).start())

    @pl.when(has_n)
    def _():
        each_tile(lambda k, t: row_copy(k, t, False).start())

    @pl.when(has_s)
    def _():
        each_tile(lambda k, t: row_copy(k, t, True).start())

    loop(1 + ready, chunks - 1, first_main)
    loop(1 + ready, 1 + early, lambda c: main_copy(c).start())

    @pl.when(has_s)
    def _():
        rows_done(row_recv_sem, False)

    @pl.when(has_n)
    def _():
        rows_done(row_recv_sem, True)

    def prepare_edge(t, carry):
        prepare(0, HALO, t)
        prepare(rows + HALO, HALO, t)
        return carry
    lax.fori_loop(0, tiles, prepare_edge, 0)

    def recv_side(side, dr, there):
        _, dest, count = ((0, rows + HALO, HALO), (0, HALO, rows), (0, 0, HALO))[dr + 1]

        @pl.when(there)
        def _():
            col_copy(side, dr).wait_recv()

        @pl.when(jnp.logical_not(there))
        def _():
            pack_recv[side, pl.ds(dest, count), :] = jnp.zeros((count, LANES), F32)

    each_side(recv_side, True)

    def unpack(first, n):
        spot = pl.ds(first + GUARD, n)
        east = pack_recv[0, pl.ds(first, n), :]
        west = pack_recv[1, pl.ds(first, n), :]
        for q in range(PACKED):
            e = pltpu.roll(east, LANES - 8 * q, 1) if q else east
            shift = (120 - 8 * q) % LANES
            w = pltpu.roll(west, shift, 1) if shift else west
            ref, index = plane_at(q, tiles, spot)
            ref[index] = jnp.where(lane < 64, e, w)

    loop(0, rows // deep, lambda i: unpack(pl.multiple_of(i * deep, deep), deep))
    unpack(rows, 2 * HALO)

    def half_east():
        tile = lax.broadcasted_iota(jnp.int32, (tiles + 1, 1, LANES), 0)
        closed = (lane3 == LANES - 1) & (
            ((tile == tiles - 1) & jnp.logical_not(has_e)) | ((tile == tiles) & jnp.logical_not(has_w)))
        return jnp.where(closed, 0.0, 0.5).astype(F32)

    def half_south(first):
        at_row = first + lax.broadcasted_iota(jnp.int32, (1, R, LANES), 1)
        closed = ((at_row == HALO - 1) & jnp.logical_not(has_n)) | (
            (at_row == HALO + rows - 1) & jnp.logical_not(has_s))
        return jnp.where(closed, 0.0, 0.5).astype(F32)

    def links_of(p, elec, first):
        if elec:
            return vert[0 if p < 2 else 2, :, at(first), :]
        if p == 0:
            return vert[0, :, at(first), :]
        if p == 3:
            return vert[2, :, at(first), :]
        return vert[p - 1, :, at(first), :] + vert[p, :, at(first), :]

    def face_rows(first, elec):
        kappa = ky if elec else cy
        here, above = half_south(first), half_south(first - 1)
        for p in range(4):
            k = kappa[p, :, at(first), :]
            south = here * (k + kappa[p, :, at(first + 1), :])
            north = above * (k + kappa[p, :, at(first - 1), :])
            east = ce[p, :, at(first), :]
            cs[p, :, at(first), :] = south
            weight = east + from_west(east) + south + north + links_of(p, elec, first) + LEAK
            rw[p, :, at(first), :] = 1.0 / weight

    def sweep(old, new, first, elec):
        for p in range(4):
            v = old[p, :, at(first), :]
            east = ce[p, :, at(first), :]
            total = east * from_east(v) + from_west(east * v)
            total = total + cs[p, :, at(first), :] * old[p, :, at(first + 1), :]
            total = total + cs[p, :, at(first - 1), :] * old[p, :, at(first - 1), :]
            if elec:
                total = total + vert[0 if p < 2 else 2, :, at(first), :] * old[p ^ 1, :, at(first), :]
                if p in (1, 2):
                    total = total + load[:, at(first), :]
            else:
                if p > 0:
                    total = total + vert[p - 1, :, at(first), :] * old[p - 1, :, at(first), :]
                if p < 3:
                    total = total + vert[p, :, at(first), :] * old[p + 1, :, at(first), :]
                if p < 2:
                    total = total + src[p, :, at(first), :]
            new[p, :, at(first), :] = total * rw[p, :, at(first), :]

    def send_chunk(c, state):
        first = pl.multiple_of(c * R, R)

        def write(planes):
            for q in range(2):
                send_map[c, q * half : (q + 1) * half, :] = planes[q][:tiles].reshape(half, LANES)
            send_map[c, 2 * half : 2 * half + STRIP, :] = strip_of([planes[q][tiles] for q in range(2)])

        @pl.when(is_elec)
        def _():
            write(heat_of(state, first, 0, tiles + 1))

        @pl.when(jnp.logical_not(is_elec))
        def _():
            write((state[0, :, at(first), :], state[1, :, at(first), :]))

        map_copy(c).start()

    def map_copy(c):
        return pltpu.make_async_remote_copy(
            src_ref=send_map.at[c], dst_ref=recv_map.at[c],
            send_sem=map_send_sem.at[c], recv_sem=map_recv_sem.at[c],
            device_id={"field": 1 - field}, device_id_type=MESH,
        )

    def read_map(step, c):
        source = recv_map if step else recv_main
        strip = recv_map[c, 2 * half : 2 * half + STRIP, :] if step else recv_strip[c]
        return [
            jnp.concatenate([source[c, q * half : (q + 1) * half, :].reshape(tiles, R, LANES), edge[None]], 0)
            for q, edge in enumerate(planes_of(strip))
        ]

    first_main(0)
    first_strips()
    main_copy(0).start()
    strip_copy.start()
    first_main(chunks - 1)
    loop(1 + early, chunks, lambda c: main_copy(c).start())

    @pl.when(jnp.logical_not(is_elec))
    def _():
        def body(c, carry):
            first = pl.multiple_of(c * R, R)
            he = half_east()
            for p in range(4):
                k = cx[p, :, at(first), :]
                ce[p, :, at(first), :] = he * (k + from_east(k))
            face_rows(first - 1, False)
            return carry
        lax.fori_loop(0, chunks, body, 0)

    def advance(step, c, buffers):
        first = pl.multiple_of(c * R, R)
        (map_copy if step else main_copy)(c).wait_recv()

        @pl.when(is_elec)
        def _():
            temps = read_map(step, c)
            factor = [1.0 / (1.0 + TEMP_COEF * t) for t in temps]
            he = half_east()
            for p in range(4):
                f = factor[(0, 1, 1, 0)[p]]
                k = cx[p, :, at(first), :] * f
                ce[p, :, at(first), :] = he * (k + from_east(k))
                ky[p, :, at(first), :] = cy[p, :, at(first), :] * f
            face_rows(first - 1, True)
            for s in range(SWEEPS):
                sweep(buffers[s], buffers[s + 1], first - 1 - s, True)

        @pl.when(jnp.logical_not(is_elec))
        def _():
            joule = read_map(step, c)
            if step == 0:
                tile = lax.broadcasted_iota(jnp.int32, (tiles + 1, 1, LANES), 0)
                last = (tile == tiles - 1) & (lane3 == LANES - 1)
                joule = [jnp.where(last, pltpu.roll(j[tiles:], 7, 2), j) for j in joule]
            src[0, :, at(first), :] = joule[0]
            src[1, :, at(first), :] = joule[1] + load[:, at(first), :]
            for s in range(SWEEPS):
                sweep(buffers[s], buffers[s + 1], first - 1 - s, False)

    strip_copy.wait_recv()

    def step_one(c, carry):
        @pl.when(c < chunks)
        def _():
            advance(0, c, (x, y, z, y, z))

        @pl.when(c > 0)
        def _():
            send_chunk(c - 1, z)
        return carry
    lax.fori_loop(0, chunks + 1, step_one, 0)

    def out_copy(c, t):
        return pltpu.make_async_copy(
            x.at[:, t, pl.ds(pl.multiple_of(c * R + GUARD + HALO, 8), R), :],
            out.at[0, :, pl.ds(pl.multiple_of(c * R, R), R), lanes_of(t)],
            out_sem.at[0],
        )

    def step_two(c, carry):
        advance(1, c, (z, y, x, y, x))

        @pl.when(c > 0)
        def _():
            for t in range(tiles):
                out_copy(c - 1, t).start()
        return carry
    lax.fori_loop(0, chunks, step_two, 0)

    wait_for(out, out_sem.at[0])
    wait_for(send_main, main_send_sem.at[0])
    strip_copy.wait_send()
    loop(0, chunks, lambda c: map_copy(c).wait_send())

    @pl.when(has_n)
    def _():
        rows_done(row_send_sem, False)

    @pl.when(has_s)
    def _():
        rows_done(row_send_sem, True)

    def sent_side(side, dr, there):
        @pl.when(there)
        def _():
            col_copy(side, dr).wait_send()

    each_side(sent_side, False)


def shards(grid_rows, grid_cols, *args):
    rows, cols = args[0].shape[2], args[0].shape[3]
    tiles = cols // LANES
    wide = rows + 2 * HALO
    chunks = wide // R
    tall = wide + 2 * GUARD
    field = pltpu.VMEM((4, tiles + 1, tall, LANES), F32)
    dma = pltpu.SemaphoreType.DMA
    hbm = pl.BlockSpec(memory_space=pl.ANY)
    return pl.pallas_call(
        functools.partial(kernel, grid_rows, grid_cols),
        name="coupled_sweeps",
        out_shape=jax.ShapeDtypeStruct(args[0].shape, F32),
        in_specs=[hbm] * 5 + [pl.BlockSpec(memory_space=pltpu.SMEM), hbm],
        out_specs=hbm,
        scratch_shapes=[
            *[field] * 9,
            pltpu.VMEM((3, tiles + 1, tall, LANES), F32),
            pltpu.VMEM((tiles + 1, tall, LANES), F32),
            pltpu.VMEM((2, tiles + 1, tall, LANES), F32),
            pltpu.VMEM((tiles, wide, LANES), F32),
            pltpu.VMEM((tiles, wide, LANES), jnp.int32),
            pltpu.VMEM((3, tiles, wide, LANES), jnp.int32),
            *[pltpu.VMEM((chunks, 2 * tiles * R, LANES), F32)] * 2,
            *[pltpu.VMEM((chunks, STRIP, LANES), F32)] * 2,
            *[pltpu.VMEM((chunks, 2 * tiles * R + STRIP, LANES), F32)] * 2,
            pltpu.VMEM((2, rows, LANES), F32),
            pltpu.VMEM((2, wide, LANES), F32),
            dma((6,)), dma((2, 6)), dma((2, 6)), dma((2, 3)), dma((2, 3)),
            dma((1,)), dma((chunks,)), dma((2,)), dma((chunks,)), dma((chunks,)), dma((1,)),
        ],
        compiler_params=pltpu.CompilerParams(
            collective_id=0, has_side_effects=True, vmem_limit_bytes=60 * 1024 * 1024
        ),
    )(*args)


def solution(mesh):
    return jax.shard_map(
        functools.partial(shards, mesh.shape["row"], mesh.shape["col"]),
        mesh=mesh,
        in_specs=(
            P("field", None, "row", "col"),
            P("field", None, "row", "col"),
            P("field", None, "row", "col"),
            P("field", "row", "col"),
            P("field", "row", "col"),
            P("field", None),
            P("field", None, "row", "col"),
        ),
        out_specs=P("field", None, "row", "col"),
        check_vma=False,
    )
```
